512 devices in a mesh: pb: 16 (over y, x_lo), item: 32 (over x_hi, z, core).
Axes of the slice: x: 4 (x_hi: 2, x_lo: 2; x = x_hi * 2 + x_lo), y: 8, z: 8, core: 2. Of those that a mesh axis runs over, the one named last changes fastest.
Arguments:
- queries: bfloat16 [8192, 512], P(('pb', 'item')), may hold values from -2 to 2
- gate_query: bfloat16 [8192, 64], P(('pb', 'item')), may hold values from -6 to 250
- items: bfloat16 [16384, 512], P(('item', 'pb')), may hold values from -2 to 2
- gate_items: bfloat16 [16384, 64], P(('item', 'pb')), may hold values from -6 to 6
- slot_tiles: int32 [16, 192], P('pb', 'item'), may hold values from -1 to 15, as said below
- d_scores: bfloat16 [16, 192, 128, 128], P('pb', 'item'), may hold values from -6 to 6
Outputs:
- grad_queries: bfloat16 [8192, 512], P(('pb', 'item'))
- grad_gate_query: float32 [8192, 64], P(('pb', 'item'))
- grad_items: bfloat16 [16384, 512], P(('item', 'pb'))
- grad_gate_items: float32 [16384, 64], P(('item', 'pb'))
The draws below stay inside these ranges and needn't reach their ends.
Inputs may be any that keep to these rules, and one draw needn't show every extreme that they name: `slot_tiles`: each device's row of slots names distinct tiles, live ones first and -1 after them. Devices (p, j) and (p, j + 32 / 2) form a pair: either one of them has all 6 slots live and the other exactly one, or both have between 1 and 3 live slots. Device (0, 0) has all 6 live.
All inputs are finite; a program needn't handle non-finite values.
Results may differ from the reference program's by a relative error of at most 0.0049.
Values may be sent and summed in bfloat16 or wider, within the bound.
No kernel may reach another device: no remote copies, remote signals or barrier semaphores. Data moves between devices by JAX's collectives and lax.ppermute only.
A program may use at most 64 MiB of HBM per device.

```python
import jax
import jax.numpy as jnp
from jax import lax

E = 64
KQ = 8
KI = 8
C = 64
TILE = 128
QB_DEV = 4
IT_DEV = 4
SLOTS = 6
NQ = 8192
NI = 16384
N_PB = 16
N_ITEM = 32


def draw_gate_query(key, part):
    subkeys = jax.random.split(key, 1)
    drawn = jnp.clip(1.5 * jax.random.normal(subkeys[0], (NQ, C), jnp.float32), -6.0, 6.0)
    return drawn.astype(jnp.bfloat16)


def draw_slot_tiles(key, part):
    devices_all = N_PB * N_ITEM
    half_item = N_ITEM // 2
    tile_total = QB_DEV * IT_DEV
    light_top = max(SLOTS // 2, 1)
    subkeys = jax.random.split(key, 5)
    pair_kind = jax.random.randint(subkeys[0], (N_PB, half_item), 0, 4)
    pair_kind = pair_kind.at[0, 0].set(0)
    full_side = jax.random.randint(subkeys[1], (N_PB, half_item), 0, 2)
    full_side = full_side.at[0, 0].set(0)
    light_low = jax.random.randint(subkeys[2], (N_PB, half_item), 1, light_top + 1)
    light_high = jax.random.randint(subkeys[3], (N_PB, half_item), 1, light_top + 1)
    skewed = pair_kind == 0
    count_low = jnp.where(skewed, jnp.where(full_side == 0, SLOTS, 1), light_low)
    count_high = jnp.where(skewed, jnp.where(full_side == 1, SLOTS, 1), light_high)
    counts = jnp.concatenate([count_low, count_high], axis=1).reshape(devices_all)
    scores = jax.random.randint(subkeys[4], (devices_all, tile_total), 0, 1048576) * tile_total + jnp.arange(tile_total)[None, :]
    order = jnp.argsort(scores, axis=1, stable=True)[:, :SLOTS]
    places = jnp.arange(SLOTS)[None, :]
    chosen = jnp.where(places < counts[:, None], order, -1)
    return chosen.reshape(N_PB, N_ITEM * SLOTS).astype(jnp.int32)


def levels(rng, shape, cuts, low, high):
    def one(dim, parts):
        heights = jax.random.uniform(jax.random.fold_in(jax.random.fold_in(rng, 6), dim), (parts,), jnp.float32, low / len(cuts), high / len(cuts))
        return jnp.repeat(jnp.exp(heights), shape[dim] // parts).reshape((-1,) + (1,) * (len(shape) - dim - 1))

    level = one(*cuts[0])
    for cut in cuts[1:]:
        level = level * one(*cut)
    return level


def normal_values(key, shape, spread, reach, pieces=(), kind=jnp.bfloat16):
    values = jax.random.normal(key, shape, jnp.float32) * spread
    if len(pieces) > 0:
        values = levels(key, shape, pieces, -0.22, 0.18) * values
    return jnp.clip(values, min=-reach, max=reach).astype(kind)


def setup_inputs(seed: int = 0) -> dict:
    key_of = jax.random.split(jax.random.key(seed), 7)
    return {
        "queries": normal_values(key_of[0], (NQ, KQ * E), 0.35, 2.0, ((0, 512),)),
        "gate_query": draw_gate_query(jax.random.fold_in(key_of[6], 71), 0),
        "items": normal_values(key_of[2], (NI, KI * E), 0.35, 2.0, ((0, 512),)),
        "gate_items": normal_values(key_of[3], (NI, C), 1.5, 6.0, ((0, 512),)),
        "slot_tiles": draw_slot_tiles(jax.random.fold_in(key_of[6], 71), 0),
        "d_scores": normal_values(key_of[5], (N_PB, N_ITEM * SLOTS, TILE, TILE), 1.0, 6.0, ((0, 16), (1, 32))),
    }


def tile_grads(query_tile, query_gate, item_tile, item_gate, cotangent):
    extent = query_tile.shape[0]
    query_parts = query_tile.astype(jnp.float32).reshape(extent, KQ, E)
    item_parts = item_tile.astype(jnp.float32).reshape(extent, KI, E)
    logits = jnp.einsum("qae,ibe->abqi", query_parts, item_parts).reshape(KQ * KI, extent, extent)
    gates = query_gate.astype(jnp.float32).T[:, :, None] + item_gate.astype(jnp.float32).T[:, None, :]
    weights = jax.nn.softmax(gates, axis=0)
    score = jnp.sum(weights * logits, axis=0)
    upstream = cotangent.astype(jnp.float32)[None]
    logit_grad = (upstream * weights).astype(jnp.bfloat16).astype(jnp.float32)
    gate_grad = upstream * weights * (logits - score[None])
    logit_parts = logit_grad.reshape(KQ, KI, extent, extent)
    query_grad = jnp.einsum("abqi,ibe->qae", logit_parts, item_parts).reshape(extent, KQ * E)
    item_grad = jnp.einsum("abqi,qae->ibe", logit_parts, query_parts).reshape(extent, KI * E)
    return query_grad, jnp.sum(gate_grad, axis=2).T, item_grad, jnp.sum(gate_grad, axis=1).T


def reference(queries, gate_query, items, gate_items, slot_tiles, d_scores):
    query_rows = TILE * QB_DEV
    item_rows = TILE * IT_DEV
    flat_ids = slot_tiles.reshape(-1).astype(jnp.int32)
    flat_cot = d_scores.reshape(-1, TILE, TILE)
    flat_index = jnp.arange(flat_ids.shape[0], dtype=jnp.int32)
    totals = (jnp.zeros(queries.shape, jnp.float32), jnp.zeros(gate_query.shape, jnp.float32),
              jnp.zeros(items.shape, jnp.float32), jnp.zeros(gate_items.shape, jnp.float32))

    def visit(carry, inputs):
        tile_id, position, cotangent = inputs
        device = position // SLOTS
        pb_index = device // N_ITEM
        item_index = device % N_ITEM
        safe_id = jnp.maximum(tile_id, 0)
        query_start = (pb_index * query_rows + (safe_id // IT_DEV) * TILE).astype(jnp.int32)
        item_start = (item_index * item_rows + (safe_id % IT_DEV) * TILE).astype(jnp.int32)

        def work(current):
            grads = tile_grads(lax.dynamic_slice_in_dim(queries, query_start, TILE, 0),
                               lax.dynamic_slice_in_dim(gate_query, query_start, TILE, 0),
                               lax.dynamic_slice_in_dim(items, item_start, TILE, 0),
                               lax.dynamic_slice_in_dim(gate_items, item_start, TILE, 0), cotangent)
            starts = (query_start, query_start, item_start, item_start)
            return tuple(lax.dynamic_update_slice_in_dim(total, lax.dynamic_slice_in_dim(total, start, TILE, 0) + update, start, 0)
                         for total, update, start in zip(current, grads, starts))

        return lax.cond(tile_id >= 0, work, lambda current: current, carry), None

    totals, unused = lax.scan(visit, totals, (flat_ids, flat_index, flat_cot))
    return (totals[0].astype(jnp.bfloat16), totals[1], totals[2].astype(jnp.bfloat16), totals[3])
```

```python
import jax
import jax.numpy as jnp
from jax import lax
from jax.sharding import PartitionSpec as P

E = 64
KQ = 8
KI = 8


def tile_grads(query_tile, query_gate, item_tile, item_gate, cotangent):
    extent = query_tile.shape[0]
    query_parts = query_tile.reshape(extent, KQ, E)
    item_parts = item_tile.reshape(extent, KI, E)
    logits = jnp.einsum(
        "qae,ibe->abqi", query_parts, item_parts, preferred_element_type=jnp.float32
    ).reshape(KQ * KI, extent, extent)
    gates = (
        query_gate.astype(jnp.float32).T[:, :, None] + item_gate.astype(jnp.float32).T[:, None, :]
    )
    weights = jax.nn.softmax(gates, axis=0)
    score = jnp.sum(weights * logits, axis=0)
    upstream = cotangent.astype(jnp.float32)[None]
    logit_grad = (upstream * weights).astype(jnp.bfloat16)
    gate_grad = upstream * weights * (logits - score[None])
    logit_parts = logit_grad.reshape(KQ, KI, extent, extent)
    query_grad = jnp.einsum(
        "abqi,ibe->qae", logit_parts, item_parts, preferred_element_type=jnp.float32
    ).reshape(extent, KQ * E)
    item_grad = jnp.einsum(
        "abqi,qae->ibe", logit_parts, query_parts, preferred_element_type=jnp.float32
    ).reshape(extent, KI * E)
    return (query_grad, jnp.sum(gate_grad, axis=2).T, item_grad, jnp.sum(gate_grad, axis=1).T)


def on_device(queries, gate_query, items, gate_items, slot_tiles, d_scores):
    def fetch(rows, gates, axis):
        width = rows.shape[1]
        packed = jnp.concatenate([rows, gates], axis=1)
        copies = jnp.tile(packed, (lax.axis_size(axis), 1))
        whole = lax.all_to_all(copies, axis, 0, 0, tiled=True)
        return whole[:, :width], whole[:, width:]

    def give(rows, gates, axis):
        width = rows.shape[1]
        packed = jnp.concatenate([rows, gates], axis=1).astype(jnp.bfloat16)
        terms = lax.all_to_all(packed, axis, 0, 0, tiled=True)
        terms = terms.reshape(lax.axis_size(axis), -1, packed.shape[1])
        total = jnp.sum(terms.astype(jnp.float32), axis=0)
        return total[:, :width].astype(jnp.bfloat16), total[:, width:]

    block_queries, block_gates = fetch(queries, gate_query, "item")
    shard_items, shard_gates = fetch(items, gate_items, "pb")
    extent = d_scores.shape[-1]
    tile_ids = slot_tiles.reshape(-1)
    cotangents = d_scores.reshape(-1, extent, extent)
    slot_count = tile_ids.shape[0]
    item_blocks = shard_items.shape[0] // extent

    def anchors(tile_id):
        safe_id = jnp.maximum(tile_id, 0)
        return (safe_id // item_blocks * extent, safe_id % item_blocks * extent)

    def operands(tile_id):
        query_start, item_start = anchors(tile_id)
        return (
            lax.dynamic_slice_in_dim(block_queries, query_start, extent, 0),
            lax.dynamic_slice_in_dim(block_gates, query_start, extent, 0),
            lax.dynamic_slice_in_dim(shard_items, item_start, extent, 0),
            lax.dynamic_slice_in_dim(shard_gates, item_start, extent, 0),
        )

    def accumulate(current, tile_id, grads):
        query_start, item_start = anchors(tile_id)
        starts = (query_start, query_start, item_start, item_start)
        return tuple(
            (
                lax.dynamic_update_slice_in_dim(
                    total, lax.dynamic_slice_in_dim(total, start, extent, 0) + update, start, 0
                )
                for total, update, start in zip(current, grads, starts)
            )
        )

    totals = (
        jnp.zeros(block_queries.shape, jnp.float32),
        jnp.zeros(block_gates.shape, jnp.float32),
        jnp.zeros(shard_items.shape, jnp.float32),
        jnp.zeros(shard_gates.shape, jnp.float32),
    )

    def home_step(position, current):
        tile_id = tile_ids[position]

        def work(state):
            return accumulate(state, tile_id, tile_grads(*operands(tile_id), cotangents[position]))

        return lax.cond(tile_id >= 0, work, lambda state: state, current)

    totals = lax.fori_loop(0, slot_count, home_step, totals)
    query_sum, query_gate_sum = give(totals[0], totals[1], "item")
    item_sum, item_gate_sum = give(totals[2], totals[3], "pb")
    return query_sum, query_gate_sum, item_sum, item_gate_sum


def solution(mesh):
    return jax.shard_map(
        on_device,
        mesh=mesh,
        in_specs=(
            P(("pb", "item"), None),
            P(("pb", "item"), None),
            P(("item", "pb"), None),
            P(("item", "pb"), None),
            P("pb", "item"),
            P("pb", "item", None, None),
        ),
        out_specs=(
            P(("pb", "item"), None),
            P(("pb", "item"), None),
            P(("item", "pb"), None),
            P(("item", "pb"), None),
        ),
        check_vma=False,
    )
```

```python
import jax
import jax.numpy as jnp
from jax import lax
from jax.experimental import pallas as pl
from jax.experimental.pallas import tpu as pltpu
from jax.sharding import PartitionSpec as P

E = 64
KQ = 8
KI = 8
F32 = jnp.float32
BF = jnp.bfloat16
LANES_OF_BOTH = (((1,), (1,)), ((), ()))


def split(x):
    high = x.astype(BF)
    return high, (x - high.astype(F32)).astype(BF)


def dot(a, b):
    return jnp.dot(a, b, preferred_element_type=F32)


def dot_lanes(a, b):
    return lax.dot_general(a, b, LANES_OF_BOTH, preferred_element_type=F32)


def tile_kernel(
    ids, q_ref, i_ref, t_ref, gq_ref, gi_ref,
    qt, it, eqt, eit, vt, xt, tile_t, n_q, n_i, n_0, ft, fit, acc_q, acc_i, weight,
):
    rows = q_ref.shape[0]
    cols = i_ref.shape[0]
    extent = t_ref.shape[-1]
    width = KQ * E
    comps = KQ * KI
    blocks = cols // extent
    step = 2 * E
    chunk = KI * step

    tile_t[...] = jnp.zeros_like(tile_t)
    for slot in range(t_ref.shape[0]):
        tile_id = ids[slot]

        @pl.when(tile_id >= 0)
        def _():
            tile_t[tile_id] = t_ref[slot].astype(F32)

    gates = q_ref[:, width:].astype(F32)
    eq = jnp.exp(gates - jnp.max(gates, axis=1, keepdims=True))
    gates_t = gates.T
    eqt[...] = jnp.exp(gates_t - jnp.max(gates_t, axis=0, keepdims=True))
    eit[...] = jnp.exp(i_ref[:, width:].astype(F32).T)
    qt[...] = q_ref[:, :width].astype(F32).T
    it[...] = i_ref[:, :width].astype(F32).T

    eq_hi, eq_mid = split(eq)
    eq_lo = (eq - eq_hi.astype(F32) - eq_mid.astype(F32)).astype(BF)
    ei_hi, ei_lo = split(eit[...])
    eqt_hi, eqt_lo = split(eqt[...])
    norm = dot(
        jnp.concatenate([eq_hi, eq_hi, eq_mid], axis=1),
        jnp.concatenate([ei_hi, ei_lo, ei_hi], axis=0),
    )
    parts = jnp.concatenate([eq_hi, eq_mid, eq_lo], axis=1)
    part_row = lax.broadcasted_iota(jnp.int32, (3 * comps, chunk), 0) % comps
    part_lane = lax.broadcasted_iota(jnp.int32, (3 * comps, chunk), 1)
    lane_comp = (part_lane // E) % 2 * KI + part_lane // step

    n_0[...] = jnp.zeros_like(n_0)
    n_q[...] = jnp.zeros_like(n_q)
    n_i[...] = jnp.zeros_like(n_i)

    def spread(ap, carry):
        pick = jnp.where(part_row == lane_comp + 2 * KI * ap, 1.0, 0.0).astype(BF)
        scale = dot(parts, pick)
        own = q_ref[:, pl.ds(pl.multiple_of(ap * step, step), step)].astype(F32)
        x_hi, x_lo = split(scale * jnp.concatenate([own] * KI, axis=1))
        lows = []
        highs = []
        for b in range(KI):
            for half in range(2):
                comp = (2 * ap + half) * KI + b
                v = it[b * E:(b + 1) * E, :] * eit[pl.ds(comp, 1), :]
                v_hi, v_lo = split(v)
                highs.append(v_hi)
                lows.append(v_lo)
                at = pl.multiple_of(ap * chunk + b * step + half * E, E)
                a_at = pl.multiple_of((2 * ap + half) * E, E)
                x = qt[pl.ds(a_at, E), :] * eqt[pl.ds(comp, 1), :]
                xt[pl.ds(at, E), :] = x.astype(BF)
        v_hi = jnp.concatenate(highs, axis=0)
        v_lo = jnp.concatenate(lows, axis=0)
        vt[pl.ds(pl.multiple_of(ap * chunk, chunk), chunk), :] = v_hi
        n_0[...] += dot(x_hi, v_hi)
        n_q[...] += dot(x_lo, v_hi)
        n_i[...] += dot(x_hi, v_lo)
        return carry

    lax.fori_loop(0, KQ // 2, spread, 0)

    lines = []
    for r in range(rows // extent):
        lines.append(
            jnp.concatenate([tile_t[r * blocks + c] for c in range(blocks)], axis=1)
        )
    inverse = 1.0 / norm
    weight[...] = (jnp.concatenate(lines, axis=0) * inverse).astype(BF)
    rounded = weight[...].astype(F32) * inverse
    whole = n_0[...]
    wq_hi, wq_lo = split(rounded * (whole + n_q[...]))
    wi_hi, wi_lo = split(rounded * (whole + n_i[...]))
    mean_q = dot_lanes(ei_hi, wq_hi) + dot_lanes(ei_lo, wq_hi) + dot_lanes(ei_hi, wq_lo)
    mean_i = dot(eqt_hi, wi_hi) + dot(eqt_lo, wi_hi) + dot(eqt_hi, wi_lo)

    acc_i[...] = jnp.zeros_like(acc_i)

    def collect(ap, carry):
        at = pl.ds(pl.multiple_of(ap * chunk, chunk), chunk)
        u = dot_lanes(vt[at, :], weight[...])
        w = dot(xt[at, :], weight[...])
        for half in range(2):
            a = 2 * ap + half
            a_rows = pl.ds(pl.multiple_of(a * E, E), E)
            own = qt[a_rows, :]
            total = jnp.zeros((E, rows), F32)
            sums_q = []
            sums_i = []
            for b in range(KI):
                low = b * step + half * E
                comp = a * KI + b
                u_part = u[low:low + E, :]
                w_part = w[low:low + E, :]
                total += u_part * eqt[pl.ds(comp, 1), :]
                acc_i[b * E:(b + 1) * E, :] += w_part * eit[pl.ds(comp, 1), :]
                sums_q.append(jnp.sum(u_part * own, axis=0, keepdims=True))
                sums_i.append(jnp.sum(w_part * it[b * E:(b + 1) * E, :], axis=0, keepdims=True))
            acc_q[a_rows, :] = total
            comp_rows = pl.ds(pl.multiple_of(a * KI, KI), KI)
            ft[comp_rows, :] = jnp.concatenate(sums_q, axis=0)
            fit[comp_rows, :] = jnp.concatenate(sums_i, axis=0)
        return carry

    lax.fori_loop(0, KQ // 2, collect, 0)

    gq_ref[:, :width] = acc_q[...].T.astype(BF)
    gi_ref[:, :width] = acc_i[...].T.astype(BF)
    gq_ref[:, width:] = (eqt[...] * (ft[...] - mean_q)).T.astype(BF)
    gi_ref[:, width:] = (eit[...] * (fit[...] - mean_i)).T.astype(BF)


def tile_grads(tile_ids, cotangents, block, shard, interpret=False):
    rows, packed = block.shape
    cols = shard.shape[0]
    width = KQ * E
    comps = KQ * KI
    extent = cotangents.shape[-1]
    vmem = pl.BlockSpec(memory_space=pltpu.VMEM)
    return pl.pallas_call(
        tile_kernel,
        out_shape=(
            jax.ShapeDtypeStruct((rows, packed), BF),
            jax.ShapeDtypeStruct((cols, packed), BF),
        ),
        in_specs=[pl.BlockSpec(memory_space=pltpu.SMEM), vmem, vmem, vmem],
        out_specs=(vmem, vmem),
        scratch_shapes=[
            pltpu.VMEM((width, rows), F32),
            pltpu.VMEM((width, cols), F32),
            pltpu.VMEM((comps, rows), F32),
            pltpu.VMEM((comps, cols), F32),
            pltpu.VMEM((comps * E, cols), BF),
            pltpu.VMEM((comps * E, rows), BF),
            pltpu.VMEM((rows * cols // extent**2, extent, extent), F32),
            pltpu.VMEM((rows, cols), F32),
            pltpu.VMEM((rows, cols), F32),
            pltpu.VMEM((rows, cols), F32),
            pltpu.VMEM((comps, rows), F32),
            pltpu.VMEM((comps, cols), F32),
            pltpu.VMEM((width, rows), F32),
            pltpu.VMEM((width, cols), F32),
            pltpu.VMEM((rows, cols), BF),
        ],
        compiler_params=pltpu.CompilerParams(vmem_limit_bytes=56 * 2**20),
        interpret=interpret,
    )(tile_ids, block, shard, cotangents)


def fetch(rows, gates, axis):
    packed = jnp.concatenate([rows, gates], axis=1)
    copies = jnp.tile(packed, (lax.axis_size(axis), 1))
    return lax.all_to_all(copies, axis, 0, 0, tiled=True)


def give(packed, width, axis):
    terms = lax.all_to_all(packed, axis, 0, 0, tiled=True)
    terms = terms.reshape(lax.axis_size(axis), -1, packed.shape[1])
    total = jnp.sum(terms.astype(F32), axis=0)
    return total[:, :width].astype(BF), total[:, width:]


def on_device(queries, gate_query, items, gate_items, slot_tiles, d_scores):
    width = queries.shape[1]
    extent = d_scores.shape[-1]
    block = fetch(queries, gate_query, "item")
    shard = fetch(items, gate_items, "pb")
    for_block, for_shard = tile_grads(
        slot_tiles.reshape(-1), d_scores.reshape(-1, extent, extent), block, shard
    )
    query_sum, query_gate_sum = give(for_block, width, "item")
    item_sum, item_gate_sum = give(for_shard, width, "pb")
    return query_sum, query_gate_sum, item_sum, item_gate_sum


def solution(mesh):
    return jax.shard_map(
        on_device,
        mesh=mesh,
        in_specs=(
            P(("pb", "item"), None),
            P(("pb", "item"), None),
            P(("item", "pb"), None),
            P(("item", "pb"), None),
            P("pb", "item"),
            P("pb", "item", None, None),
        ),
        out_specs=(
            P(("pb", "item"), None),
            P(("pb", "item"), None),
            P(("item", "pb"), None),
            P(("item", "pb"), None),
        ),
        check_vma=False,
    )
```

```python
import jax
import jax.numpy as jnp
from jax import lax
from jax.experimental import pallas as pl
from jax.experimental.pallas import tpu as pltpu
from jax.sharding import Mesh
from jax.sharding import PartitionSpec as P


E = 64
KQ = 8
KI = 8
F32 = jnp.float32
BF = jnp.bfloat16
LANES_OF_BOTH = (((1,), (1,)), ((), ()))


def split(x):
    high = x.astype(BF)
    return high, (x - high.astype(F32)).astype(BF)


def dot(a, b):
    return jnp.dot(a, b, preferred_element_type=F32)


def dot_lanes(a, b):
    return lax.dot_general(a, b, LANES_OF_BOTH, preferred_element_type=F32)


def tile_kernel(
    ids, q_own, q_other, i_own, i_other, t_ref, q_keep, q_send, i_keep, i_send,
    q_ref, i_ref, gq_ref, gi_ref,
    qt, it, eqt, eit, vt, xt, tile_t, n_q, n_i, n_0, ft, fit, acc_q, acc_i, weight,
):
    core = ids[t_ref.shape[0]]
    side = ids[t_ref.shape[0] + 1]

    def places(index, whole, half):
        size = half.shape[1]
        for g in range(half.shape[0]):
            mine = pl.multiple_of(g * 2 * size + index * size, size)
            theirs = pl.multiple_of(g * 2 * size + (1 - index) * size, size)
            yield g, whole.at[pl.ds(mine, size), :], whole.at[pl.ds(theirs, size), :]

    for g, mine, theirs in places(core, q_ref, q_own):
        mine[...] = q_own[g]
        theirs[...] = q_other[g]
    for g, mine, theirs in places(side, i_ref, i_own):
        mine[...] = i_own[g]
        theirs[...] = i_other[g]

    rows = q_ref.shape[0]
    cols = i_ref.shape[0]
    extent = t_ref.shape[-1]
    width = KQ * E
    comps = KQ * KI
    blocks = cols // extent
    step = 2 * E
    chunk = KI * step

    tile_t[...] = jnp.zeros_like(tile_t)
    for slot in range(t_ref.shape[0]):
        tile_id = ids[slot]

        @pl.when(tile_id >= 0)
        def _():
            tile_t[tile_id] = t_ref[slot].astype(F32)

    gates = q_ref[:, width:].astype(F32)
    eq = jnp.exp(gates - jnp.max(gates, axis=1, keepdims=True))
    gates_t = gates.T
    eqt[...] = jnp.exp(gates_t - jnp.max(gates_t, axis=0, keepdims=True))
    eit[...] = jnp.exp(i_ref[:, width:].astype(F32).T)
    qt[...] = q_ref[:, :width].astype(F32).T
    it[...] = i_ref[:, :width].astype(F32).T

    eq_hi, eq_mid = split(eq)
    eq_lo = (eq - eq_hi.astype(F32) - eq_mid.astype(F32)).astype(BF)
    ei_hi, ei_lo = split(eit[...])
    eqt_hi, eqt_lo = split(eqt[...])
    norm = dot(
        jnp.concatenate([eq_hi, eq_hi, eq_mid], axis=1),
        jnp.concatenate([ei_hi, ei_lo, ei_hi], axis=0),
    )
    parts = jnp.concatenate([eq_hi, eq_mid, eq_lo], axis=1)
    part_row = lax.broadcasted_iota(jnp.int32, (3 * comps, chunk), 0) % comps
    part_lane = lax.broadcasted_iota(jnp.int32, (3 * comps, chunk), 1)
    lane_comp = (part_lane // E) % 2 * KI + part_lane // step

    n_0[...] = jnp.zeros_like(n_0)
    n_q[...] = jnp.zeros_like(n_q)
    n_i[...] = jnp.zeros_like(n_i)

    def spread(ap, carry):
        pick = jnp.where(part_row == lane_comp + 2 * KI * ap, 1.0, 0.0).astype(BF)
        scale = dot(parts, pick)
        own = q_ref[:, pl.ds(pl.multiple_of(ap * step, step), step)].astype(F32)
        x_hi, x_lo = split(scale * jnp.concatenate([own] * KI, axis=1))
        lows = []
        highs = []
        for b in range(KI):
            for half in range(2):
                comp = (2 * ap + half) * KI + b
                v = it[b * E:(b + 1) * E, :] * eit[pl.ds(comp, 1), :]
                v_hi, v_lo = split(v)
                highs.append(v_hi)
                lows.append(v_lo)
                at = pl.multiple_of(ap * chunk + b * step + half * E, E)
                a_at = pl.multiple_of((2 * ap + half) * E, E)
                x = qt[pl.ds(a_at, E), :] * eqt[pl.ds(comp, 1), :]
                xt[pl.ds(at, E), :] = x.astype(BF)
        v_hi = jnp.concatenate(highs, axis=0)
        v_lo = jnp.concatenate(lows, axis=0)
        vt[pl.ds(pl.multiple_of(ap * chunk, chunk), chunk), :] = v_hi
        n_0[...] += dot(x_hi, v_hi)
        n_q[...] += dot(x_lo, v_hi)
        n_i[...] += dot(x_hi, v_lo)
        return carry

    lax.fori_loop(0, KQ // 2, spread, 0)

    lines = []
    for r in range(rows // extent):
        lines.append(
            jnp.concatenate([tile_t[r * blocks + c] for c in range(blocks)], axis=1)
        )
    inverse = 1.0 / norm
    weight[...] = (jnp.concatenate(lines, axis=0) * inverse).astype(BF)
    rounded = weight[...].astype(F32) * inverse
    whole = n_0[...]
    wq_hi, wq_lo = split(rounded * (whole + n_q[...]))
    wi_hi, wi_lo = split(rounded * (whole + n_i[...]))
    mean_q = dot_lanes(ei_hi, wq_hi) + dot_lanes(ei_lo, wq_hi) + dot_lanes(ei_hi, wq_lo)
    mean_i = dot(eqt_hi, wi_hi) + dot(eqt_lo, wi_hi) + dot(eqt_hi, wi_lo)

    acc_i[...] = jnp.zeros_like(acc_i)

    def collect(ap, carry):
        at = pl.ds(pl.multiple_of(ap * chunk, chunk), chunk)
        u = dot_lanes(vt[at, :], weight[...])
        w = dot(xt[at, :], weight[...])
        for half in range(2):
            a = 2 * ap + half
            a_rows = pl.ds(pl.multiple_of(a * E, E), E)
            own = qt[a_rows, :]
            total = jnp.zeros((E, rows), F32)
            sums_q = []
            sums_i = []
            for b in range(KI):
                low = b * step + half * E
                comp = a * KI + b
                u_part = u[low:low + E, :]
                w_part = w[low:low + E, :]
                total += u_part * eqt[pl.ds(comp, 1), :]
                acc_i[b * E:(b + 1) * E, :] += w_part * eit[pl.ds(comp, 1), :]
                sums_q.append(jnp.sum(u_part * own, axis=0, keepdims=True))
                sums_i.append(jnp.sum(w_part * it[b * E:(b + 1) * E, :], axis=0, keepdims=True))
            acc_q[a_rows, :] = total
            comp_rows = pl.ds(pl.multiple_of(a * KI, KI), KI)
            ft[comp_rows, :] = jnp.concatenate(sums_q, axis=0)
            fit[comp_rows, :] = jnp.concatenate(sums_i, axis=0)
        return carry

    lax.fori_loop(0, KQ // 2, collect, 0)

    gq_ref[:, :width] = acc_q[...].T
    gq_ref[:, width:] = (eqt[...] * (ft[...] - mean_q)).T
    for g, mine, theirs in places(core, gq_ref, q_keep):
        q_keep[g] = mine[...]
        q_send[g] = theirs[...].astype(BF)
    gi_ref[:, :width] = acc_i[...].T
    gi_ref[:, width:] = (eit[...] * (fit[...] - mean_i)).T
    for g, mine, theirs in places(side, gi_ref, i_keep):
        i_keep[g] = mine[...]
        i_send[g] = theirs[...].astype(BF)


def tile_grads(scalars, cotangents, q_own, q_other, i_own, i_other, interpret=False):
    packed = q_own.shape[-1]
    rows = 2 * q_own.shape[0] * q_own.shape[1]
    cols = 2 * i_own.shape[0] * i_own.shape[1]
    width = KQ * E
    comps = KQ * KI
    extent = cotangents.shape[-1]
    vmem = pl.BlockSpec(memory_space=pltpu.VMEM)
    return pl.pallas_call(
        tile_kernel,
        out_shape=(
            jax.ShapeDtypeStruct(q_own.shape, F32),
            jax.ShapeDtypeStruct(q_own.shape, BF),
            jax.ShapeDtypeStruct(i_own.shape, F32),
            jax.ShapeDtypeStruct(i_own.shape, BF),
        ),
        in_specs=[pl.BlockSpec(memory_space=pltpu.SMEM)] + [vmem] * 5,
        out_specs=(vmem,) * 4,
        scratch_shapes=[
            pltpu.VMEM((rows, packed), BF),
            pltpu.VMEM((cols, packed), BF),
            pltpu.VMEM((rows, packed), F32),
            pltpu.VMEM((cols, packed), F32),
            pltpu.VMEM((width, rows), F32),
            pltpu.VMEM((width, cols), F32),
            pltpu.VMEM((comps, rows), F32),
            pltpu.VMEM((comps, cols), F32),
            pltpu.VMEM((comps * E, cols), BF),
            pltpu.VMEM((comps * E, rows), BF),
            pltpu.VMEM((rows * cols // extent**2, extent, extent), F32),
            pltpu.VMEM((rows, cols), F32),
            pltpu.VMEM((rows, cols), F32),
            pltpu.VMEM((rows, cols), F32),
            pltpu.VMEM((comps, rows), F32),
            pltpu.VMEM((comps, cols), F32),
            pltpu.VMEM((width, rows), F32),
            pltpu.VMEM((width, cols), F32),
            pltpu.VMEM((rows, cols), BF),
        ],
        compiler_params=pltpu.CompilerParams(vmem_limit_bytes=40 * 2**20),
        interpret=interpret,
    )(scalars, q_own, q_other, i_own, i_other, cotangents)


SWAP = [(0, 1), (1, 0)]
AXES = (("y", 8), ("x_lo", 2), ("x_hi", 2), ("z", 8), ("core", 2))
PB = ("y", "x_lo")
ITEM = ("x_hi", "z", "core")


def fetch(rows, gates, axes):
    packed = jnp.concatenate([rows, gates], axis=1)
    copies = jnp.broadcast_to(packed[None], (lax.axis_size(axes),) + packed.shape)
    return lax.all_to_all(copies, axes, 0, 0)


def give(keep, send, pair, axes, width):
    got = lax.ppermute(send, pair, SWAP)
    total = (keep + got.astype(F32)).astype(BF)
    terms = lax.all_to_all(total, axes, 0, 0)
    total = jnp.sum(terms.astype(F32), axis=0)
    return total[:, :width].astype(BF), total[:, width:]


def on_device(queries, gate_query, items, gate_items, slot_tiles, d_scores):
    width = queries.shape[1]
    extent = d_scores.shape[-1]
    i_own = fetch(items, gate_items, ("y",))
    i_other = lax.ppermute(i_own, "x_lo", SWAP)
    q_own = fetch(queries, gate_query, ("x_hi", "z"))
    q_other = lax.ppermute(q_own, "core", SWAP)
    place = [lax.axis_index("core")[None], lax.axis_index("x_lo")[None]]
    scalars = jnp.concatenate([slot_tiles.reshape(-1)] + place)
    cotangents = d_scores.reshape(-1, extent, extent)
    q_keep, q_send, i_keep, i_send = tile_grads(
        scalars, cotangents, q_own, q_other, i_own, i_other
    )
    query_sum, query_gate_sum = give(q_keep, q_send, "core", ("x_hi", "z"), width)
    item_sum, item_gate_sum = give(i_keep, i_send, "x_lo", ("y",), width)
    return query_sum, query_gate_sum, item_sum, item_gate_sum


def solution(mesh):
    fine = Mesh(
        mesh.devices.reshape([size for name, size in AXES]), [name for name, size in AXES]
    )
    block = P(PB + ITEM, None)
    shard = P(ITEM + PB, None)
    return jax.shard_map(
        on_device,
        mesh=fine,
        in_specs=(block, block, shard, shard, P(PB, ITEM), P(PB, ITEM, None, None)),
        out_specs=(block, block, shard, shard),
        check_vma=False,
    )
```

```python
import jax
import jax.numpy as jnp
from jax import lax
from jax.experimental import pallas as pl
from jax.experimental.pallas import tpu as pltpu
from jax.sharding import Mesh
from jax.sharding import PartitionSpec as P


E = 64
KQ = 8
KI = 8
F32 = jnp.float32
BF = jnp.bfloat16
LANES_OF_BOTH = (((1,), (1,)), ((), ()))


def split(x):
    high = x.astype(BF)
    return high, (x - high.astype(F32)).astype(BF)


def dot(a, b):
    return jnp.dot(a, b, preferred_element_type=F32)


def dot_lanes(a, b):
    return lax.dot_general(a, b, LANES_OF_BOTH, preferred_element_type=F32)


def tile_kernel(
    ids, q_own, q_other, i_own, i_other, t_ref, q_keep, q_send, i_keep, i_send,
    q_ref, i_ref, gq_ref, gi_ref,
    qt, it, eqt, eit, vt, xt, tile_t, n_0, ft, fit, acc_q, acc_i, weight,
):
    core = ids[t_ref.shape[0]]
    side = ids[t_ref.shape[0] + 1]

    def places(index, whole, half):
        size = half.shape[1]
        for g in range(half.shape[0]):
            mine = pl.multiple_of(g * 2 * size + index * size, size)
            theirs = pl.multiple_of(g * 2 * size + (1 - index) * size, size)
            yield g, whole.at[pl.ds(mine, size), :], whole.at[pl.ds(theirs, size), :]

    for g, mine, theirs in places(core, q_ref, q_own):
        mine[...] = q_own[g]
        theirs[...] = q_other[g]
    for g, mine, theirs in places(side, i_ref, i_own):
        mine[...] = i_own[g]
        theirs[...] = i_other[g]

    rows = q_ref.shape[0]
    cols = i_ref.shape[0]
    extent = t_ref.shape[-1]
    width = KQ * E
    comps = KQ * KI
    blocks = cols // extent
    step = 2 * E
    chunk = KI * step

    tile_t[...] = jnp.zeros_like(tile_t)
    for slot in range(t_ref.shape[0]):
        tile_id = ids[slot]

        @pl.when(tile_id >= 0)
        def _():
            tile_t[tile_id] = t_ref[slot].astype(F32)

    gates = q_ref[:, width:].astype(F32)
    eq = jnp.exp(gates - jnp.max(gates, axis=1, keepdims=True))
    gates_t = gates.T
    eqt[...] = jnp.exp(gates_t - jnp.max(gates_t, axis=0, keepdims=True))
    eit[...] = jnp.exp(i_ref[:, width:].astype(F32).T)
    qt[...] = q_ref[:, :width].astype(F32).T
    it[...] = i_ref[:, :width].astype(F32).T

    eq_hi, eq_mid = split(eq)
    eq_lo = (eq - eq_hi.astype(F32) - eq_mid.astype(F32)).astype(BF)
    ei_hi, ei_lo = split(eit[...])
    eqt_hi, eqt_lo = split(eqt[...])
    norm = dot(
        jnp.concatenate([eq_hi, eq_hi, eq_mid], axis=1),
        jnp.concatenate([ei_hi, ei_lo, ei_hi], axis=0),
    )
    parts = jnp.concatenate([eq_hi, eq_mid, eq_lo], axis=1)
    part_row = lax.broadcasted_iota(jnp.int32, (3 * comps, chunk), 0) % comps
    part_lane = lax.broadcasted_iota(jnp.int32, (3 * comps, chunk), 1)
    lane_comp = (part_lane // E) % 2 * KI + part_lane // step

    n_0[...] = jnp.zeros_like(n_0)

    def spread(ap, carry):
        pick = jnp.where(part_row == lane_comp + 2 * KI * ap, 1.0, 0.0).astype(BF)
        scale = dot(parts, pick)
        own = q_ref[:, pl.ds(pl.multiple_of(ap * step, step), step)].astype(F32)
        x_rows = (scale * jnp.concatenate([own] * KI, axis=1)).astype(BF)
        for b in range(KI):
            for half in range(2):
                comp = (2 * ap + half) * KI + b
                at = pl.multiple_of(ap * chunk + b * step + half * E, E)
                a_at = pl.multiple_of((2 * ap + half) * E, E)
                x = qt[pl.ds(a_at, E), :] * eqt[pl.ds(comp, 1), :]
                xt[pl.ds(at, E), :] = x.astype(BF)
                v = it[b * E:(b + 1) * E, :] * eit[pl.ds(comp, 1), :]
                vt[pl.ds(at, E), :] = v.astype(BF)
        n_0[...] += dot(x_rows, vt[pl.ds(pl.multiple_of(ap * chunk, chunk), chunk), :])
        return carry

    lax.fori_loop(0, KQ // 2, spread, 0)

    lines = []
    for r in range(rows // extent):
        lines.append(
            jnp.concatenate([tile_t[r * blocks + c] for c in range(blocks)], axis=1)
        )
    inverse = 1.0 / norm
    weight[...] = (jnp.concatenate(lines, axis=0) * inverse).astype(BF)
    w_hi, w_lo = split(weight[...].astype(F32) * inverse * n_0[...])
    mean_q = dot_lanes(ei_hi, w_hi) + dot_lanes(ei_lo, w_hi) + dot_lanes(ei_hi, w_lo)
    mean_i = dot(eqt_hi, w_hi) + dot(eqt_lo, w_hi) + dot(eqt_hi, w_lo)

    acc_i[...] = jnp.zeros_like(acc_i)

    def collect(ap, carry):
        at = pl.ds(pl.multiple_of(ap * chunk, chunk), chunk)
        u = dot_lanes(vt[at, :], weight[...])
        w = dot(xt[at, :], weight[...])
        for half in range(2):
            a = 2 * ap + half
            a_rows = pl.ds(pl.multiple_of(a * E, E), E)
            total = jnp.zeros((E, rows), F32)
            sums_q = []
            sums_i = []
            for b in range(KI):
                low = b * step + half * E
                comp = a * KI + b
                u_part = u[low:low + E, :]
                w_part = w[low:low + E, :]
                total += u_part * eqt[pl.ds(comp, 1), :]
                acc_i[b * E:(b + 1) * E, :] += w_part * eit[pl.ds(comp, 1), :]
                kept = pl.ds(pl.multiple_of(ap * chunk + low, E), E)
                x = xt[kept, :].astype(F32)
                v = vt[kept, :].astype(F32)
                sums_q.append(jnp.sum(u_part * x, axis=0, keepdims=True))
                sums_i.append(jnp.sum(w_part * v, axis=0, keepdims=True))
            acc_q[a_rows, :] = total
            comp_rows = pl.ds(pl.multiple_of(a * KI, KI), KI)
            ft[comp_rows, :] = jnp.concatenate(sums_q, axis=0)
            fit[comp_rows, :] = jnp.concatenate(sums_i, axis=0)
        return carry

    lax.fori_loop(0, KQ // 2, collect, 0)

    gq_ref[:, :width] = acc_q[...].T
    gq_ref[:, width:] = (ft[...] - eqt[...] * mean_q).T
    for g, mine, theirs in places(core, gq_ref, q_keep):
        q_keep[g] = mine[...]
        q_send[g] = theirs[...].astype(BF)
    gi_ref[:, :width] = acc_i[...].T
    gi_ref[:, width:] = (fit[...] - eit[...] * mean_i).T
    for g, mine, theirs in places(side, gi_ref, i_keep):
        i_keep[g] = mine[...]
        i_send[g] = theirs[...].astype(BF)


def tile_grads(scalars, cotangents, q_own, q_other, i_own, i_other, interpret=False):
    packed = q_own.shape[-1]
    rows = 2 * q_own.shape[0] * q_own.shape[1]
    cols = 2 * i_own.shape[0] * i_own.shape[1]
    width = KQ * E
    comps = KQ * KI
    extent = cotangents.shape[-1]
    vmem = pl.BlockSpec(memory_space=pltpu.VMEM)
    return pl.pallas_call(
        tile_kernel,
        out_shape=(
            jax.ShapeDtypeStruct(q_own.shape, F32),
            jax.ShapeDtypeStruct(q_own.shape, BF),
            jax.ShapeDtypeStruct(i_own.shape, F32),
            jax.ShapeDtypeStruct(i_own.shape, BF),
        ),
        in_specs=[pl.BlockSpec(memory_space=pltpu.SMEM)] + [vmem] * 5,
        out_specs=(vmem,) * 4,
        scratch_shapes=[
            pltpu.VMEM((rows, packed), BF),
            pltpu.VMEM((cols, packed), BF),
            pltpu.VMEM((rows, packed), F32),
            pltpu.VMEM((cols, packed), F32),
            pltpu.VMEM((width, rows), F32),
            pltpu.VMEM((width, cols), F32),
            pltpu.VMEM((comps, rows), F32),
            pltpu.VMEM((comps, cols), F32),
            pltpu.VMEM((comps * E, cols), BF),
            pltpu.VMEM((comps * E, rows), BF),
            pltpu.VMEM((rows * cols // extent**2, extent, extent), F32),
            pltpu.VMEM((rows, cols), F32),
            pltpu.VMEM((comps, rows), F32),
            pltpu.VMEM((comps, cols), F32),
            pltpu.VMEM((width, rows), F32),
            pltpu.VMEM((width, cols), F32),
            pltpu.VMEM((rows, cols), BF),
        ],
        compiler_params=pltpu.CompilerParams(vmem_limit_bytes=40 * 2**20),
        interpret=interpret,
    )(scalars, q_own, q_other, i_own, i_other, cotangents)


SWAP = [(0, 1), (1, 0)]
AXES = (("y", 8), ("x_lo", 2), ("x_hi", 2), ("z", 8), ("core", 2))
PB = ("y", "x_lo")
ITEM = ("x_hi", "z", "core")


def fetch(rows, gates, axes):
    packed = jnp.concatenate([rows, gates], axis=1)
    copies = jnp.broadcast_to(packed[None], (lax.axis_size(axes),) + packed.shape)
    return lax.all_to_all(copies, axes, 0, 0)


def give(keep, send, pair, axes, width):
    got = lax.ppermute(send, pair, SWAP)
    total = (keep + got.astype(F32)).astype(BF)
    terms = lax.all_to_all(total, axes, 0, 0)
    total = jnp.sum(terms.astype(F32), axis=0)
    return total[:, :width].astype(BF), total[:, width:]


def on_device(queries, gate_query, items, gate_items, slot_tiles, d_scores):
    width = queries.shape[1]
    extent = d_scores.shape[-1]
    i_own = fetch(items, gate_items, ("y",))
    i_other = lax.ppermute(i_own, "x_lo", SWAP)
    q_own = fetch(queries, gate_query, ("x_hi", "z"))
    q_other = lax.ppermute(q_own, "core", SWAP)
    place = [lax.axis_index("core")[None], lax.axis_index("x_lo")[None]]
    scalars = jnp.concatenate([slot_tiles.reshape(-1)] + place)
    cotangents = d_scores.reshape(-1, extent, extent)
    q_keep, q_send, i_keep, i_send = tile_grads(
        scalars, cotangents, q_own, q_other, i_own, i_other
    )
    query_sum, query_gate_sum = give(q_keep, q_send, "core", ("x_hi", "z"), width)
    item_sum, item_gate_sum = give(i_keep, i_send, "x_lo", ("y",), width)
    return query_sum, query_gate_sum, item_sum, item_gate_sum


def solution(mesh):
    fine = Mesh(
        mesh.devices.reshape([size for name, size in AXES]), [name for name, size in AXES]
    )
    block = P(PB + ITEM, None)
    shard = P(ITEM + PB, None)
    return jax.shard_map(
        on_device,
        mesh=fine,
        in_specs=(block, block, shard, shard, P(PB, ITEM), P(PB, ITEM, None, None)),
        out_specs=(block, block, shard, shard),
        check_vma=False,
    )
```

```python
import jax
import jax.numpy as jnp
from jax import lax
from jax.experimental import pallas as pl
from jax.experimental.pallas import tpu as pltpu
from jax.sharding import Mesh
from jax.sharding import PartitionSpec as P


E = 64
KQ = 8
KI = 8
F32 = jnp.float32
BF = jnp.bfloat16
LANES_OF_BOTH = (((1,), (1,)), ((), ()))


def split(x):
    high = x.astype(BF)
    return high, (x - high.astype(F32)).astype(BF)


def dot(a, b):
    return jnp.dot(a, b, preferred_element_type=F32)


def dot_lanes(a, b):
    return lax.dot_general(a, b, LANES_OF_BOTH, preferred_element_type=F32)


def tile_kernel(
    ids, q_own, q_other, i_own, i_other, t_ref, q_keep, q_send, i_keep, i_send,
    q_ref, q_gate, i_gate, out, gate,
    qt, it, eqt, eit, vt, xt, tile_t, n_0, ft, fit, acc_q, acc_i, weight,
):
    core = ids[t_ref.shape[0]]
    side = ids[t_ref.shape[0] + 1]

    rows = q_ref.shape[1]
    cols = i_gate.shape[0]
    extent = t_ref.shape[-1]
    lanes = q_ref.shape[2]
    chunks = KQ * E // lanes
    comps = KQ * KI
    blocks = cols // extent
    step = 2 * E
    chunk = KI * step

    def places(index, parts, size):
        for g in range(parts):
            yield g, pl.multiple_of(g * 2 * size + index * size, size)

    def unpack(index, parts, embeds, gates):
        size = parts.shape[1] * lanes // (chunks * lanes + comps)
        half = size // 2
        for g, at in places(index, parts.shape[0], size):
            for j in range(chunks):
                embeds[j, pl.ds(at, size), :] = parts[g, j * size:(j + 1) * size, :].astype(
                    embeds.dtype
                )
            tail = parts[g, chunks * size:, :].astype(F32)
            gates[pl.ds(at, half), :] = tail[:, :comps]
            gates[pl.ds(pl.multiple_of(at + half, half), half), :] = tail[:, comps:]

    def pack(index, parts):
        size = parts.shape[1] * lanes // (chunks * lanes + comps)
        half = size // 2
        for g, at in places(index, parts.shape[0], size):
            for j in range(chunks):
                parts[g, j * size:(j + 1) * size, :] = out[j, pl.ds(at, size), :].astype(
                    parts.dtype
                )
            first = gate[pl.ds(at, half), :]
            last = gate[pl.ds(pl.multiple_of(at + half, half), half), :]
            parts[g, chunks * size:, :] = jnp.concatenate([first, last], axis=1).astype(
                parts.dtype
            )

    unpack(core, q_own, q_ref, q_gate)
    unpack(1 - core, q_other, q_ref, q_gate)
    unpack(side, i_own, out, i_gate)
    unpack(1 - side, i_other, out, i_gate)

    tile_t[...] = jnp.zeros_like(tile_t)
    for slot in range(t_ref.shape[0]):
        tile_id = ids[slot]

        @pl.when(tile_id >= 0)
        def _():
            tile_t[tile_id] = t_ref[slot].astype(F32)

    gates = q_gate[...]
    eq = jnp.exp(gates - jnp.max(gates, axis=1, keepdims=True))
    gates_t = gates.T
    eqt[...] = jnp.exp(gates_t - jnp.max(gates_t, axis=0, keepdims=True))
    eit[...] = jnp.exp(i_gate[...].T)
    for j in range(chunks):
        qt[j * lanes:(j + 1) * lanes, :] = q_ref[j].astype(F32).T
        it[j * lanes:(j + 1) * lanes, :] = out[j].T

    eq_hi, eq_mid = split(eq)
    eq_lo = (eq - eq_hi.astype(F32) - eq_mid.astype(F32)).astype(BF)
    ei_hi, ei_lo = split(eit[...])
    eqt_hi, eqt_lo = split(eqt[...])
    norm = dot(
        jnp.concatenate([eq_hi, eq_hi, eq_mid], axis=1),
        jnp.concatenate([ei_hi, ei_lo, ei_hi], axis=0),
    )
    parts = jnp.concatenate([eq_hi, eq_mid, eq_lo], axis=1)
    part_row = lax.broadcasted_iota(jnp.int32, (3 * comps, chunk), 0) % comps
    part_lane = lax.broadcasted_iota(jnp.int32, (3 * comps, chunk), 1)
    lane_comp = (part_lane // E) % 2 * KI + part_lane // step

    n_0[...] = jnp.zeros_like(n_0)

    def spread(ap, carry):
        pick = jnp.where(part_row == lane_comp + 2 * KI * ap, 1.0, 0.0).astype(BF)
        scale = dot(parts, pick)
        own = q_ref[ap].astype(F32)
        x_rows = (scale * jnp.concatenate([own] * KI, axis=1)).astype(BF)
        for b in range(KI):
            for half in range(2):
                comp = (2 * ap + half) * KI + b
                at = pl.multiple_of(ap * chunk + b * step + half * E, E)
                a_at = pl.multiple_of((2 * ap + half) * E, E)
                x = qt[pl.ds(a_at, E), :] * eqt[pl.ds(comp, 1), :]
                xt[pl.ds(at, E), :] = x.astype(BF)
                v = it[b * E:(b + 1) * E, :] * eit[pl.ds(comp, 1), :]
                vt[pl.ds(at, E), :] = v.astype(BF)
        n_0[...] += dot(x_rows, vt[pl.ds(pl.multiple_of(ap * chunk, chunk), chunk), :])
        return carry

    lax.fori_loop(0, KQ // 2, spread, 0)

    lines = []
    for r in range(rows // extent):
        lines.append(
            jnp.concatenate([tile_t[r * blocks + c] for c in range(blocks)], axis=1)
        )
    inverse = 1.0 / norm
    weight[...] = (jnp.concatenate(lines, axis=0) * inverse).astype(BF)
    w_hi, w_lo = split(weight[...].astype(F32) * inverse * n_0[...])
    mean_q = dot_lanes(ei_hi, w_hi) + dot_lanes(ei_lo, w_hi) + dot_lanes(ei_hi, w_lo)
    mean_i = dot(eqt_hi, w_hi) + dot(eqt_lo, w_hi) + dot(eqt_hi, w_lo)

    acc_i[...] = jnp.zeros_like(acc_i)

    def collect(ap, carry):
        at = pl.ds(pl.multiple_of(ap * chunk, chunk), chunk)
        u = dot_lanes(vt[at, :], weight[...])
        w = dot(xt[at, :], weight[...])
        for half in range(2):
            a = 2 * ap + half
            a_rows = pl.ds(pl.multiple_of(a * E, E), E)
            total = jnp.zeros((E, rows), F32)
            sums_q = []
            sums_i = []
            for b in range(KI):
                low = b * step + half * E
                comp = a * KI + b
                u_part = u[low:low + E, :]
                w_part = w[low:low + E, :]
                total += u_part * eqt[pl.ds(comp, 1), :]
                acc_i[b * E:(b + 1) * E, :] += w_part * eit[pl.ds(comp, 1), :]
                kept = pl.ds(pl.multiple_of(ap * chunk + low, E), E)
                x = xt[kept, :].astype(F32)
                v = vt[kept, :].astype(F32)
                sums_q.append(jnp.sum(u_part * x, axis=0, keepdims=True))
                sums_i.append(jnp.sum(w_part * v, axis=0, keepdims=True))
            acc_q[a_rows, :] = total
            comp_rows = pl.ds(pl.multiple_of(a * KI, KI), KI)
            ft[comp_rows, :] = jnp.concatenate(sums_q, axis=0)
            fit[comp_rows, :] = jnp.concatenate(sums_i, axis=0)
        return carry

    lax.fori_loop(0, KQ // 2, collect, 0)

    for j in range(chunks):
        out[j] = acc_q[j * lanes:(j + 1) * lanes, :].T
    gate[...] = (ft[...] - eqt[...] * mean_q).T
    pack(core, q_keep)
    pack(1 - core, q_send)
    for j in range(chunks):
        out[j] = acc_i[j * lanes:(j + 1) * lanes, :].T
    gate[...] = (fit[...] - eit[...] * mean_i).T
    pack(side, i_keep)
    pack(1 - side, i_send)


def total_kernel(terms, embeds, gates):
    total = jnp.sum(terms[...].astype(F32), axis=0)
    size, width = embeds.shape
    lanes = total.shape[1]
    half = size // 2
    comps = gates.shape[1]
    for j in range(width // lanes):
        embeds[:, j * lanes:(j + 1) * lanes] = total[j * size:(j + 1) * size, :].astype(BF)
    tail = total[width // lanes * size:, :]
    gates[:half, :] = tail[:, :comps]
    gates[half:, :] = tail[:, comps:]


def tile_grads(scalars, cotangents, q_own, q_other, i_own, i_other, interpret=False):
    lanes = q_own.shape[-1]
    width = KQ * E
    comps = KQ * KI
    rows = 2 * q_own.shape[0] * q_own.shape[1] * lanes // (width + comps)
    cols = 2 * i_own.shape[0] * i_own.shape[1] * lanes // (width + comps)
    extent = cotangents.shape[-1]
    vmem = pl.BlockSpec(memory_space=pltpu.VMEM)
    return pl.pallas_call(
        tile_kernel,
        out_shape=(
            jax.ShapeDtypeStruct(q_own.shape, F32),
            jax.ShapeDtypeStruct(q_own.shape, BF),
            jax.ShapeDtypeStruct(i_own.shape, F32),
            jax.ShapeDtypeStruct(i_own.shape, BF),
        ),
        in_specs=[pl.BlockSpec(memory_space=pltpu.SMEM)] + [vmem] * 5,
        out_specs=(vmem,) * 4,
        scratch_shapes=[
            pltpu.VMEM((width // lanes, rows, lanes), BF),
            pltpu.VMEM((rows, comps), F32),
            pltpu.VMEM((cols, comps), F32),
            pltpu.VMEM((width // lanes, rows, lanes), F32),
            pltpu.VMEM((rows, comps), F32),
            pltpu.VMEM((width, rows), F32),
            pltpu.VMEM((width, cols), F32),
            pltpu.VMEM((comps, rows), F32),
            pltpu.VMEM((comps, cols), F32),
            pltpu.VMEM((comps * E, cols), BF),
            pltpu.VMEM((comps * E, rows), BF),
            pltpu.VMEM((rows * cols // extent**2, extent, extent), F32),
            pltpu.VMEM((rows, cols), F32),
            pltpu.VMEM((comps, rows), F32),
            pltpu.VMEM((comps, cols), F32),
            pltpu.VMEM((width, rows), F32),
            pltpu.VMEM((width, cols), F32),
            pltpu.VMEM((rows, cols), BF),
        ],
        compiler_params=pltpu.CompilerParams(vmem_limit_bytes=40 * 2**20),
        interpret=interpret,
    )(scalars, q_own, q_other, i_own, i_other, cotangents)


SWAP = [(0, 1), (1, 0)]
AXES = (("y", 8), ("x_lo", 2), ("x_hi", 2), ("z", 8), ("core", 2))
PB = ("y", "x_lo")
ITEM = ("x_hi", "z", "core")


def copy_kernel(embeds, gates, copies):
    size, width = embeds.shape
    lanes = copies.shape[2]
    half = size // 2
    values = gates[...].astype(F32)
    tail = jnp.concatenate([values[:half], values[half:]], axis=1).astype(BF)
    for g in range(copies.shape[0]):
        for j in range(width // lanes):
            copies[g, j * size:(j + 1) * size, :] = embeds[:, j * lanes:(j + 1) * lanes]
        copies[g, width // lanes * size:, :] = tail


def fetch(rows, gates, axes):
    lanes = 2 * gates.shape[1]
    packed = rows.shape[0] * (rows.shape[1] + gates.shape[1]) // lanes
    vmem = pl.BlockSpec(memory_space=pltpu.VMEM)
    copies = pl.pallas_call(
        copy_kernel,
        out_shape=jax.ShapeDtypeStruct((lax.axis_size(axes), packed, lanes), BF),
        in_specs=[vmem, vmem],
        out_specs=vmem,
        compiler_params=pltpu.CompilerParams(vmem_limit_bytes=8 * 2**20),
    )(rows, gates)
    return lax.all_to_all(copies, axes, 0, 0)


def give(keep, send, pair, axes, width):
    got = lax.ppermute(send, pair, SWAP)
    total = (keep + got.astype(F32)).astype(BF)
    terms = lax.all_to_all(total, axes, 0, 0)
    comps = KQ * KI
    size = terms.shape[1] * terms.shape[2] // (width + comps)
    vmem = pl.BlockSpec(memory_space=pltpu.VMEM)
    return pl.pallas_call(
        total_kernel,
        out_shape=(
            jax.ShapeDtypeStruct((size, width), BF),
            jax.ShapeDtypeStruct((size, comps), F32),
        ),
        in_specs=[vmem],
        out_specs=(vmem, vmem),
        compiler_params=pltpu.CompilerParams(vmem_limit_bytes=8 * 2**20),
    )(terms)


def on_device(queries, gate_query, items, gate_items, slot_tiles, d_scores):
    width = queries.shape[1]
    extent = d_scores.shape[-1]
    i_own = fetch(items, gate_items, ("y",))
    i_other = lax.ppermute(i_own, "x_lo", SWAP)
    q_own = fetch(queries, gate_query, ("x_hi", "z"))
    q_other = lax.ppermute(q_own, "core", SWAP)
    place = [lax.axis_index("core")[None], lax.axis_index("x_lo")[None]]
    scalars = jnp.concatenate([slot_tiles.reshape(-1)] + place)
    cotangents = d_scores.reshape(-1, extent, extent)
    q_keep, q_send, i_keep, i_send = tile_grads(
        scalars, cotangents, q_own, q_other, i_own, i_other
    )
    query_sum, query_gate_sum = give(q_keep, q_send, "core", ("x_hi", "z"), width)
    item_sum, item_gate_sum = give(i_keep, i_send, "x_lo", ("y",), width)
    return query_sum, query_gate_sum, item_sum, item_gate_sum


def solution(mesh):
    fine = Mesh(
        mesh.devices.reshape([size for name, size in AXES]), [name for name, size in AXES]
    )
    block = P(PB + ITEM, None)
    shard = P(ITEM + PB, None)
    return jax.shard_map(
        on_device,
        mesh=fine,
        in_specs=(block, block, shard, shard, P(PB, ITEM), P(PB, ITEM, None, None)),
        out_specs=(block, block, shard, shard),
        check_vma=False,
    )
```
